32 devices in a mesh: dp: 4 (over y, x), seq: 8 (over z, core).
Axes of the slice: x: 2, y: 2, z: 4, core: 2. Of those that a mesh axis runs over, the one named last changes fastest.
Arguments:
- hidden_in: bfloat16 [8, 1024, 1024], P('dp', 'seq'), may hold values from -6 to 6
- out_grad: bfloat16 [8, 1024, 1024], P('dp', 'seq'), may hold values from -6 to 6
- prefix_len: int32 [8], P('dp'), may hold values from 102 to 512, as said below
- alibi_slopes: float32 [16], replicated, may hold values from 0.0009765625 to 0.25
- ln1_gain: float32 [1024], P(('dp', 'seq')), may hold values from 0.5 to 1.5
- ln1_shift: float32 [1024], P(('dp', 'seq')), may hold values from -1.25 to 1.25
- qkv_weight: float32 [1024, 3072], P(('dp', 'seq')), may hold values from -0.1875 to 0.1875
- qkv_bias: float32 [3072], P(('dp', 'seq')), may hold values from -1.25 to 1.25
- dense_weight: float32 [1024, 1024], P(('dp', 'seq')), may hold values from -0.75 to 0.75
- dense_bias: float32 [1024], P(('dp', 'seq')), may hold values from -1.25 to 1.25
- ln2_gain: float32 [1024], P(('dp', 'seq')), may hold values from 0.5 to 1.5
- ln2_shift: float32 [1024], P(('dp', 'seq')), may hold values from -1.25 to 1.25
- fc1_weight: float32 [1024, 4096], P(('dp', 'seq')), may hold values from -0.1875 to 0.1875
- fc1_bias: float32 [4096], P(('dp', 'seq')), may hold values from -1.25 to 1.25
- fc2_weight: float32 [4096, 1024], P(('dp', 'seq')), may hold values from -0.125 to 0.125
- fc2_bias: float32 [1024], P(('dp', 'seq')), may hold values from -1.25 to 1.25
Outputs:
- layer_out: bfloat16 [8, 1024, 1024], P('dp', 'seq')
- input_grad: bfloat16 [8, 1024, 1024], P('dp', 'seq')
- grad_ln1_gain: float32 [1024], P(('dp', 'seq'))
- grad_ln1_shift: float32 [1024], P(('dp', 'seq'))
- grad_qkv_weight: float32 [1024, 3072], P(('dp', 'seq'))
- grad_qkv_bias: float32 [3072], P(('dp', 'seq'))
- grad_dense_weight: float32 [1024, 1024], P(('dp', 'seq'))
- grad_dense_bias: float32 [1024], P(('dp', 'seq'))
- grad_ln2_gain: float32 [1024], P(('dp', 'seq'))
- grad_ln2_shift: float32 [1024], P(('dp', 'seq'))
- grad_fc1_weight: float32 [1024, 4096], P(('dp', 'seq'))
- grad_fc1_bias: float32 [4096], P(('dp', 'seq'))
- grad_fc2_weight: float32 [4096, 1024], P(('dp', 'seq'))
- grad_fc2_bias: float32 [1024], P(('dp', 'seq'))
The draws below stay inside these ranges and needn't reach their ends.
Inputs may be any that keep to these rules, and one draw needn't show every extreme that they name: prefix_len of each sequence lies between a tenth and a half of 1024; some sequence has each end.
All inputs are finite; a program needn't handle non-finite values.
Results may differ from the reference program's by a relative error of at most 0.017.
Values may be sent and summed in bfloat16 or wider, within the bound.
No kernel may reach another device: no remote copies, remote signals or barrier semaphores. Data moves between devices by JAX's collectives and lax.ppermute only.
A program may use at most 256 MiB of HBM per device.

```python
import math
import jax
import jax.numpy as jnp
from jax import lax

D = 1024
HEADS = 16
FF = 4096
HEAD_DIM = 64
LENGTH = 1024
SEQS = 8


def draw_prefix_len(key, part):
    lowest = LENGTH // 10
    highest_len = LENGTH // 2
    drawn = jax.random.randint(jax.random.fold_in(key, 11), (SEQS,), lowest, highest_len + 1)
    order = jax.random.permutation(jax.random.fold_in(key, 12), SEQS)
    drawn = drawn.at[order[0]].set(highest_len).at[order[1]].set(lowest)
    return drawn.astype(jnp.int32)


def steps_of(own_key, shape, pieces, smallest, top_value):
    def one(position, parts):
        steps = jax.random.uniform(jax.random.fold_in(jax.random.fold_in(own_key, 6), position), (parts,), jnp.float32, smallest / len(pieces), top_value / len(pieces))
        return jnp.repeat(jnp.exp(steps), shape[position] // parts).reshape((-1,) + (1,) * (len(shape) - position - 1))

    factor_of = one(*pieces[0])
    for cut in pieces[1:]:
        factor_of = factor_of * one(*cut)
    return factor_of


def normal_values(own_key, extent, scale, bound, pieces=(), kind=jnp.bfloat16):
    level = steps_of(own_key, extent, pieces, -0.22, 0.18) if pieces else 1.0
    result = jax.random.normal(own_key, extent, jnp.float32) * scale * level
    return jnp.minimum(jnp.maximum(result, -bound), bound).astype(kind)


def setup_inputs(seed: int = 0) -> dict:
    seeds = jax.random.split(jax.random.key(seed), 17)
    return {
        "hidden_in": normal_values(seeds[0], (SEQS, LENGTH, D), 1.0, 6.0, ((0, 4), (1, 8))),
        "out_grad": normal_values(seeds[1], (SEQS, LENGTH, D), 1.0, 6.0, ((0, 4), (1, 8))),
        "prefix_len": draw_prefix_len(jax.random.fold_in(seeds[16], 71), 0),
        "alibi_slopes": jnp.clip(jnp.exp(jax.random.uniform(seeds[3], (HEADS,), jnp.float32, math.log(0.0009765625), math.log(0.25))), 0.0009765625, 0.25),
        "ln1_gain": jnp.clip(1.0 + 0.1 * jax.random.normal(seeds[4], (D,), jnp.float32), 0.5, 1.5),
        "ln1_shift": normal_values(seeds[5], (D,), 0.2, 1.25, ((0, 32),), jnp.float32),
        "qkv_weight": normal_values(seeds[6], (D, 3 * D), D ** -0.5, 0.1875, ((0, 32),), jnp.float32),
        "qkv_bias": normal_values(seeds[7], (3 * D,), 0.2, 1.25, ((0, 32),), jnp.float32),
        "dense_weight": normal_values(seeds[8], (D, D), (D // 16) ** -0.5, 0.75, ((0, 32),), jnp.float32),
        "dense_bias": normal_values(seeds[9], (D,), 0.2, 1.25, ((0, 32),), jnp.float32),
        "ln2_gain": jnp.clip(1.0 + 0.1 * jax.random.normal(seeds[10], (D,), jnp.float32), 0.5, 1.5),
        "ln2_shift": normal_values(seeds[11], (D,), 0.2, 1.25, ((0, 32),), jnp.float32),
        "fc1_weight": normal_values(seeds[12], (D, FF), D ** -0.5, 0.1875, ((0, 32),), jnp.float32),
        "fc1_bias": normal_values(seeds[13], (FF,), 0.2, 1.25, ((0, 32),), jnp.float32),
        "fc2_weight": normal_values(seeds[14], (FF, D), (FF // 2) ** -0.5, 0.125, ((0, 32),), jnp.float32),
        "fc2_bias": normal_values(seeds[15], (D,), 0.2, 1.25, ((0, 32),), jnp.float32),
    }


@jax.custom_vjp
def low(v):
    return lax.optimization_barrier(v.astype(jnp.bfloat16)).astype(jnp.float32)

@jax.custom_vjp
def low_back(v):
    return v

def low_keep(v):
    return (low(v), None)

def low_pass(kept, grad):
    return (grad,)

def back_keep(v):
    return (v, None)

def back_low(kept, grad):
    return (low(grad),)
low.defvjp(low_keep, low_pass)
low_back.defvjp(back_keep, back_low)
epsilon = 1e-05
root_coef = 0.7978845608028654
cubic_coef = 0.044715

def layer_norm(values, gain_vec, shift_vec):
    centred = values - lax.optimization_barrier(jnp.mean(values, axis=-1, keepdims=True))
    spread = lax.optimization_barrier(jnp.mean(centred * centred, axis=-1, keepdims=True))
    return centred * lax.rsqrt(spread + epsilon) * gain_vec + shift_vec

def gelu_tanh(values):
    return 0.5 * values * (1.0 + jnp.tanh(root_coef * (values + cubic_coef * values * values * values)))

def highest(left_side, right_side):
    return jnp.dot(left_side, right_side, precision=lax.Precision.HIGHEST, preferred_element_type=jnp.float32)

def attend(queries, keys, values, slopes, prefix):
    length = queries.shape[0]
    block_rows = min(512, length)
    score_scale = HEAD_DIM ** (-0.5)
    key_pos = jnp.arange(length, dtype=jnp.int32)

    def one_block(block_item):
        query_blk, start_row = block_item
        query_pos = start_row + jnp.arange(block_rows, dtype=jnp.int32)
        scores = jnp.einsum('qhd,khd->hqk', query_blk, keys, precision=lax.Precision.HIGHEST) * score_scale
        distance = jnp.abs(query_pos[:, None] - key_pos[None, :]).astype(jnp.float32)
        scores = scores - slopes[:, None, None] * distance[None]
        allowed = (key_pos[None, :] <= query_pos[:, None]) | (key_pos[None, :] < prefix)
        scores = low_back(jnp.where(allowed[None], scores, -1e+30))
        probs = low(jax.nn.softmax(scores, axis=-1))
        return jnp.einsum('hqk,khd->qhd', probs, values, precision=lax.Precision.HIGHEST)
    query_blocks = queries.reshape(length // block_rows, block_rows, HEADS, HEAD_DIM)
    starts = jnp.arange(length // block_rows, dtype=jnp.int32) * block_rows
    output = lax.map(jax.checkpoint(one_block), (query_blocks, starts))
    return output.reshape(length, D)

def block_layer(hidden, params, slopes, prefix):
    gain_one, shift_one, qkv_mat, qkv_vec, dense_mat, dense_vec, gain_two, shift_two, up_mat, up_vec, down_mat, down_vec = params
    length = hidden.shape[0]
    normed = low(layer_norm(hidden, gain_one, shift_one))
    merged_qkv = highest(normed, qkv_mat) + qkv_vec
    queries = low(low_back(merged_qkv[:, :D])).reshape(length, HEADS, HEAD_DIM)
    keys = low(low_back(merged_qkv[:, D:2 * D])).reshape(length, HEADS, HEAD_DIM)
    values = low(low_back(merged_qkv[:, 2 * D:])).reshape(length, HEADS, HEAD_DIM)
    context = low(low_back(attend(queries, keys, values, slopes, prefix)))
    attn_out = low_back(highest(context, dense_mat) + dense_vec)
    second = hidden + attn_out
    normed_two = low(layer_norm(second, gain_two, shift_two))
    pre_act = low_back(highest(normed_two, up_mat) + up_vec)
    activity = low(gelu_tanh(pre_act))
    mlp_out = low_back(highest(activity, down_mat) + down_vec)
    return second + mlp_out

def reference(hidden_in, out_grad, prefix_len, alibi_slopes, ln1_gain, ln1_shift, qkv_weight, qkv_bias, dense_weight, dense_bias, ln2_gain, ln2_shift, fc1_weight, fc1_bias, fc2_weight, fc2_bias):
    params = (ln1_gain, ln1_shift, qkv_weight, qkv_bias, dense_weight, dense_bias, ln2_gain, ln2_shift, fc1_weight, fc1_bias, fc2_weight, fc2_bias)
    inputs = hidden_in.astype(jnp.float32)
    cotangent = out_grad.astype(jnp.float32)

    def whole(inputs, params):
        rounded = tuple((low(item) for item in params))

        def one_sequence(carried, seq_item):
            hidden, prefix = seq_item
            return (carried, block_layer(hidden, rounded, alibi_slopes, prefix))
        carried, outputs = lax.scan(one_sequence, jnp.zeros((), jnp.float32), (inputs, prefix_len))
        return outputs
    outputs, pullback = jax.vjp(whole, inputs, params)
    input_grads, param_grads = pullback(cotangent)
    return (outputs.astype(jnp.bfloat16), input_grads.astype(jnp.bfloat16), param_grads[0], param_grads[1], param_grads[2], param_grads[3], param_grads[4], param_grads[5], param_grads[6], param_grads[7], param_grads[8], param_grads[9], param_grads[10], param_grads[11])
```

```python
import functools
import math

import jax
import jax.numpy as jnp
from jax import lax
from jax.experimental import pallas as pl
from jax.experimental.pallas import tpu as pltpu
from jax.sharding import Mesh
from jax.sharding import PartitionSpec as P

epsilon = 1e-05
root_coef = 0.7978845608028654
cubic_coef = 0.044715


def layer_norm(values, gain_vec, shift_vec):
    centred = values - jnp.mean(values, axis=-1, keepdims=True)
    spread = jnp.mean(centred * centred, axis=-1, keepdims=True)
    return centred * lax.rsqrt(spread + epsilon) * gain_vec + shift_vec


def gelu_tanh(values):
    return (
        0.5
        * values
        * (1.0 + jnp.tanh(root_coef * (values + cubic_coef * values * values * values)))
    )


def unchanged(state_in):
    return state_in


def column_sum(values):
    return jnp.sum(values.astype(jnp.float32), axis=0)


def inner_grad(left_side, right_side):
    return jnp.einsum("rd,re->de", left_side, right_side, preferred_element_type=jnp.float32)


def back_product(grads, matrix):
    return jnp.einsum("re,de->rd", grads, matrix, preferred_element_type=jnp.float32)


def on_device(
    hidden_in,
    out_grad,
    prefix_len,
    alibi_slopes,
    ln1_gain,
    ln1_shift,
    qkv_weight,
    qkv_bias,
    dense_weight,
    dense_bias,
    ln2_gain,
    ln2_shift,
    fc1_weight,
    fc1_bias,
    fc2_weight,
    fc2_bias,
):
    masters = (
        ln1_gain,
        ln1_shift,
        qkv_weight,
        qkv_bias,
        dense_weight,
        dense_bias,
        ln2_gain,
        ln2_shift,
        fc1_weight,
        fc1_bias,
        fc2_weight,
        fc2_bias,
    )
    micro_count, local_rows, model_width = hidden_in.shape
    head_count = alibi_slopes.shape[0]
    head_dim = model_width // head_count
    score_scale = head_dim ** (-0.5)
    seq_devices = lax.axis_size("seq")
    all_devices = lax.axis_size("dp") * seq_devices
    length = local_rows * seq_devices
    first_row = lax.axis_index("seq") * local_rows
    query_pos = first_row + jnp.arange(local_rows, dtype=jnp.int32)
    grad_sums = [
        jnp.zeros((item.shape[0] * all_devices,) + item.shape[1:], jnp.float32) for item in masters
    ]
    layer_outs = []
    input_grads = []

    def biased_scores(query_heads, row_pos, key_heads, key_pos, prefix_now):
        scores = (
            jnp.einsum("qhd,khd->hqk", query_heads, key_heads, preferred_element_type=jnp.float32)
            * score_scale
        )
        distance = jnp.abs(row_pos[:, None] - key_pos[None, :]).astype(jnp.float32)
        scores = scores - alibi_slopes[:, None, None] * distance[None]
        allowed = (key_pos[None, :] <= row_pos[:, None]) | (key_pos[None, :] < prefix_now)
        return (scores, allowed[None])

    def score_grads(
        query_heads,
        ctx_grad_heads,
        log_tot,
        delta_now,
        row_pos,
        key_heads,
        value_heads,
        key_pos,
        prefix_now,
    ):
        scores, allowed = biased_scores(query_heads, row_pos, key_heads, key_pos, prefix_now)
        probs_f = jnp.where(allowed, jnp.exp(scores - log_tot[:, :, None]), 0.0)
        prob_grad = jnp.einsum(
            "qhd,khd->hqk", ctx_grad_heads, value_heads, preferred_element_type=jnp.float32
        )
        score_grad = (probs_f * (prob_grad - delta_now[:, :, None])).astype(jnp.bfloat16)
        return (probs_f, score_grad)

    for micro_idx in range(micro_count):
        shards = [item.astype(jnp.bfloat16) for item in masters]
        fwd_weights = (
            lax.all_gather(shards[0], ("dp", "seq"), axis=0, tiled=True),
            lax.all_gather(shards[1], ("dp", "seq"), axis=0, tiled=True),
            lax.all_gather(shards[2], ("dp", "seq"), axis=0, tiled=True),
            lax.all_gather(shards[3], ("dp", "seq"), axis=0, tiled=True),
            lax.all_gather(shards[4], ("dp", "seq"), axis=0, tiled=True),
            lax.all_gather(shards[5], ("dp", "seq"), axis=0, tiled=True),
            lax.all_gather(shards[6], ("dp", "seq"), axis=0, tiled=True),
            lax.all_gather(shards[7], ("dp", "seq"), axis=0, tiled=True),
            lax.all_gather(shards[8], ("dp", "seq"), axis=0, tiled=True),
            lax.all_gather(shards[9], ("dp", "seq"), axis=0, tiled=True),
            lax.all_gather(shards[10], ("dp", "seq"), axis=0, tiled=True),
            lax.all_gather(shards[11], ("dp", "seq"), axis=0, tiled=True),
        )
        (
            gain_one,
            shift_one,
            qkv_mat,
            qkv_vec,
            dense_mat,
            dense_vec,
            gain_two,
            shift_two,
            up_mat,
            up_vec,
            down_mat,
            down_vec,
        ) = fwd_weights
        prefix_now = prefix_len[micro_idx]
        key_reach = jnp.maximum(first_row + local_rows - 1, prefix_now - 1)
        hidden = hidden_in[micro_idx].astype(jnp.float32)
        normed = layer_norm(
            hidden, gain_one.astype(jnp.float32), shift_one.astype(jnp.float32)
        ).astype(jnp.bfloat16)
        merged_qkv = jnp.dot(normed, qkv_mat, preferred_element_type=jnp.float32) + qkv_vec.astype(
            jnp.float32
        )
        queries = (
            merged_qkv[:, :model_width]
            .astype(jnp.bfloat16)
            .reshape(local_rows, head_count, head_dim)
        )
        key_local = merged_qkv[:, model_width : 2 * model_width].astype(jnp.bfloat16)
        value_local = merged_qkv[:, 2 * model_width :].astype(jnp.bfloat16)
        start_state = (
            jnp.zeros((local_rows, head_count, head_dim), jnp.float32),
            jnp.full((head_count, local_rows), -1e30, jnp.float32),
            jnp.zeros((head_count, local_rows), jnp.float32),
        )
        carried = start_state
        key_piece = lax.all_gather(key_local, "seq", axis=0, tiled=True)
        value_piece = lax.all_gather(value_local, "seq", axis=0, tiled=True)
        piece_rows = key_piece.shape[0]
        block_rows = math.gcd(piece_rows, 512)

        def forward_visit(state_now, block_index):
            offset_rows = block_index * block_rows
            block_start = offset_rows

            def forward_compute(state_in):
                partial_out, running_max, running_total = state_in
                key_heads = lax.dynamic_slice_in_dim(key_piece, offset_rows, block_rows, 0).reshape(
                    block_rows, head_count, head_dim
                )
                value_heads = lax.dynamic_slice_in_dim(
                    value_piece, offset_rows, block_rows, 0
                ).reshape(block_rows, head_count, head_dim)
                key_pos = block_start + jnp.arange(block_rows, dtype=jnp.int32)
                scores, allowed = biased_scores(queries, query_pos, key_heads, key_pos, prefix_now)
                scores = jnp.where(allowed, scores, -1e30)
                new_max = jnp.maximum(running_max, jnp.max(scores, axis=-1))
                rescale = jnp.exp(running_max - new_max)
                exp_scores = jnp.where(allowed, jnp.exp(scores - new_max[:, :, None]), 0.0)
                running_total = running_total * rescale + jnp.sum(exp_scores, axis=-1)
                partial_out = partial_out * rescale.T[:, :, None] + jnp.einsum(
                    "hqk,khd->qhd",
                    exp_scores.astype(jnp.bfloat16),
                    value_heads,
                    preferred_element_type=jnp.float32,
                )
                return (partial_out, new_max, running_total)

            return (lax.cond(block_start <= key_reach, forward_compute, unchanged, state_now), None)

        carried, ignored = lax.scan(
            forward_visit, carried, jnp.arange(piece_rows // block_rows, dtype=jnp.int32)
        )
        partial_out, running_max, running_total = carried
        context_heads = partial_out / running_total.T[:, :, None]
        log_total = running_max + jnp.log(running_total)
        context = context_heads.reshape(local_rows, model_width).astype(jnp.bfloat16)
        second = (
            hidden
            + jnp.dot(context, dense_mat, preferred_element_type=jnp.float32)
            + dense_vec.astype(jnp.float32)
        )
        normed_two = layer_norm(
            second, gain_two.astype(jnp.float32), shift_two.astype(jnp.float32)
        ).astype(jnp.bfloat16)
        pre_act = jnp.dot(normed_two, up_mat, preferred_element_type=jnp.float32) + up_vec.astype(
            jnp.float32
        )
        activity = gelu_tanh(pre_act).astype(jnp.bfloat16)
        layer_outs.append(
            (
                second
                + jnp.dot(activity, down_mat, preferred_element_type=jnp.float32)
                + down_vec.astype(jnp.float32)
            ).astype(jnp.bfloat16)
        )
        again_shards = [item.astype(jnp.bfloat16) for item in masters]
        back_weights = (
            lax.all_gather(again_shards[0], ("dp", "seq"), axis=0, tiled=True),
            lax.all_gather(again_shards[1], ("dp", "seq"), axis=0, tiled=True),
            lax.all_gather(again_shards[2], ("dp", "seq"), axis=0, tiled=True),
            lax.all_gather(again_shards[3], ("dp", "seq"), axis=0, tiled=True),
            lax.all_gather(again_shards[4], ("dp", "seq"), axis=0, tiled=True),
            lax.all_gather(again_shards[5], ("dp", "seq"), axis=0, tiled=True),
            lax.all_gather(again_shards[6], ("dp", "seq"), axis=0, tiled=True),
            lax.all_gather(again_shards[7], ("dp", "seq"), axis=0, tiled=True),
            lax.all_gather(again_shards[8], ("dp", "seq"), axis=0, tiled=True),
            lax.all_gather(again_shards[9], ("dp", "seq"), axis=0, tiled=True),
            lax.all_gather(again_shards[10], ("dp", "seq"), axis=0, tiled=True),
            lax.all_gather(again_shards[11], ("dp", "seq"), axis=0, tiled=True),
        )
        (
            gain_one,
            shift_one,
            qkv_mat,
            qkv_vec,
            dense_mat,
            dense_vec,
            gain_two,
            shift_two,
            up_mat,
            up_vec,
            down_mat,
            down_vec,
        ) = back_weights
        out_cot = out_grad[micro_idx].astype(jnp.float32)
        mlp_grad = out_cot.astype(jnp.bfloat16)
        grad_sums[11] = grad_sums[11] + column_sum(mlp_grad)
        grad_sums[10] = grad_sums[10] + inner_grad(activity, mlp_grad)
        act_grad = back_product(mlp_grad, down_mat)
        ignored_out, gelu_pull = jax.vjp(gelu_tanh, pre_act)
        pre_grad = gelu_pull(act_grad)[0].astype(jnp.bfloat16)
        grad_sums[9] = grad_sums[9] + column_sum(pre_grad)
        grad_sums[8] = grad_sums[8] + inner_grad(normed_two, pre_grad)
        normed_two_grad = back_product(pre_grad, up_mat)
        ignored_two, norm_two_pull = jax.vjp(
            layer_norm, second, gain_two.astype(jnp.float32), shift_two.astype(jnp.float32)
        )
        second_norm_grad, gain_two_grad, shift_two_grad = norm_two_pull(normed_two_grad)
        grad_sums[6] = grad_sums[6] + gain_two_grad
        grad_sums[7] = grad_sums[7] + shift_two_grad
        second_grad = out_cot + second_norm_grad
        attn_grad = second_grad.astype(jnp.bfloat16)
        grad_sums[5] = grad_sums[5] + column_sum(attn_grad)
        grad_sums[4] = grad_sums[4] + inner_grad(context, attn_grad)
        context_grad = back_product(attn_grad, dense_mat).astype(jnp.bfloat16)
        context_grad_heads = context_grad.reshape(local_rows, head_count, head_dim)
        delta = jnp.einsum("qhd,qhd->hq", context_grad_heads.astype(jnp.float32), context_heads)
        query_zero = jnp.zeros((local_rows, head_count, head_dim), jnp.float32)
        back_state = (query_zero, jnp.zeros((length, 2 * model_width), jnp.float32))
        make_carried = back_state
        make_key_piece = lax.all_gather(key_local, "seq", axis=0, tiled=True)
        make_value_piece = lax.all_gather(value_local, "seq", axis=0, tiled=True)
        make_piece_rows = make_key_piece.shape[0]
        make_block_rows = math.gcd(make_piece_rows, 512)

        def make_visit(state_now, block_index):
            offset_rows = block_index * make_block_rows
            block_start = offset_rows

            def make_compute(state_in):
                key_heads = lax.dynamic_slice_in_dim(
                    make_key_piece, offset_rows, make_block_rows, 0
                ).reshape(make_block_rows, head_count, head_dim)
                value_heads = lax.dynamic_slice_in_dim(
                    make_value_piece, offset_rows, make_block_rows, 0
                ).reshape(make_block_rows, head_count, head_dim)
                key_pos = block_start + jnp.arange(make_block_rows, dtype=jnp.int32)
                probs_f, score_grad = score_grads(
                    queries,
                    context_grad_heads,
                    log_total,
                    delta,
                    query_pos,
                    key_heads,
                    value_heads,
                    key_pos,
                    prefix_now,
                )
                query_grad = (
                    state_in[0]
                    + jnp.einsum(
                        "hqk,khd->qhd", score_grad, key_heads, preferred_element_type=jnp.float32
                    )
                    * score_scale
                )
                key_grad = (
                    jnp.einsum(
                        "hqk,qhd->khd", score_grad, queries, preferred_element_type=jnp.float32
                    )
                    * score_scale
                )
                value_grad = jnp.einsum(
                    "hqk,qhd->khd",
                    probs_f.astype(jnp.bfloat16),
                    context_grad_heads,
                    preferred_element_type=jnp.float32,
                )
                update_rows = jnp.concatenate(
                    [
                        key_grad.reshape(make_block_rows, model_width),
                        value_grad.reshape(make_block_rows, model_width),
                    ],
                    axis=1,
                )
                key_value_grad = lax.dynamic_update_slice_in_dim(
                    state_in[1], update_rows, block_start, 0
                )
                return (query_grad, key_value_grad)

            return (lax.cond(block_start <= key_reach, make_compute, unchanged, state_now), None)

        make_carried, make_ignored = lax.scan(
            make_visit,
            make_carried,
            jnp.arange(make_piece_rows // make_block_rows, dtype=jnp.int32),
        )
        query_grad, key_value_grad = make_carried
        own_key_value = lax.psum_scatter(
            key_value_grad.astype(jnp.bfloat16), "seq", scatter_dimension=0, tiled=True
        ).astype(jnp.float32)
        merged_grad = jnp.concatenate(
            [query_grad.reshape(local_rows, model_width), own_key_value], axis=1
        ).astype(jnp.bfloat16)
        grad_sums[3] = grad_sums[3] + column_sum(merged_grad)
        grad_sums[2] = grad_sums[2] + inner_grad(normed, merged_grad)
        normed_grad = back_product(merged_grad, qkv_mat)
        ignored_one, norm_one_pull = jax.vjp(
            layer_norm, hidden, gain_one.astype(jnp.float32), shift_one.astype(jnp.float32)
        )
        first_norm_grad, gain_one_grad, shift_one_grad = norm_one_pull(normed_grad)
        grad_sums[0] = grad_sums[0] + gain_one_grad
        grad_sums[1] = grad_sums[1] + shift_one_grad
        input_grads.append((second_grad + first_norm_grad).astype(jnp.bfloat16))
    owned = (
        lax.psum_scatter(grad_sums[0], ("dp", "seq"), scatter_dimension=0, tiled=True),
        lax.psum_scatter(grad_sums[1], ("dp", "seq"), scatter_dimension=0, tiled=True),
        lax.psum_scatter(grad_sums[2], ("dp", "seq"), scatter_dimension=0, tiled=True),
        lax.psum_scatter(grad_sums[3], ("dp", "seq"), scatter_dimension=0, tiled=True),
        lax.psum_scatter(grad_sums[4], ("dp", "seq"), scatter_dimension=0, tiled=True),
        lax.psum_scatter(grad_sums[5], ("dp", "seq"), scatter_dimension=0, tiled=True),
        lax.psum_scatter(grad_sums[6], ("dp", "seq"), scatter_dimension=0, tiled=True),
        lax.psum_scatter(grad_sums[7], ("dp", "seq"), scatter_dimension=0, tiled=True),
        lax.psum_scatter(grad_sums[8], ("dp", "seq"), scatter_dimension=0, tiled=True),
        lax.psum_scatter(grad_sums[9], ("dp", "seq"), scatter_dimension=0, tiled=True),
        lax.psum_scatter(grad_sums[10], ("dp", "seq"), scatter_dimension=0, tiled=True),
        lax.psum_scatter(grad_sums[11], ("dp", "seq"), scatter_dimension=0, tiled=True),
    )
    return (
        jnp.stack(layer_outs),
        jnp.stack(input_grads),
        owned[0],
        owned[1],
        owned[2],
        owned[3],
        owned[4],
        owned[5],
        owned[6],
        owned[7],
        owned[8],
        owned[9],
        owned[10],
        owned[11],
    )


def general(mesh):
    placed = (
        P("dp", "seq", None),
        P("dp", "seq", None),
        P("dp"),
        P(),
        P(("dp", "seq")),
        P(("dp", "seq")),
        P(("dp", "seq"), None),
        P(("dp", "seq")),
        P(("dp", "seq"), None),
        P(("dp", "seq")),
        P(("dp", "seq")),
        P(("dp", "seq")),
        P(("dp", "seq"), None),
        P(("dp", "seq")),
        P(("dp", "seq"), None),
        P(("dp", "seq")),
    )
    return jax.shard_map(
        on_device,
        mesh=mesh,
        in_specs=placed,
        out_specs=(
            P("dp", "seq", None),
            P("dp", "seq", None),
            P(("dp", "seq")),
            P(("dp", "seq")),
            P(("dp", "seq"), None),
            P(("dp", "seq")),
            P(("dp", "seq"), None),
            P(("dp", "seq")),
            P(("dp", "seq")),
            P(("dp", "seq")),
            P(("dp", "seq"), None),
            P(("dp", "seq")),
            P(("dp", "seq"), None),
            P(("dp", "seq")),
        ),
        check_vma=False,
    )


bf16 = jnp.bfloat16
f32 = jnp.float32
AXES = ("y", "x", "z", "c")
PLACE = (0, 2, 1, 3)
QROWS = 256


def dot_nt(a, b):
    return lax.dot_general(a, b, (((1,), (1,)), ((), ())), preferred_element_type=f32)


def dot_nn(a, b):
    return lax.dot_general(a, b, (((1,), (0,)), ((), ())), preferred_element_type=f32)


def dot_tn(a, b):
    return lax.dot_general(a, b, (((0,), (0,)), ((), ())), preferred_element_type=f32)


def augmented(head, keys, queries, slopes, first):
    rows = keys.shape[0]
    lane_k = lax.broadcasted_iota(jnp.int32, (rows, 128), 1)
    pos = lax.broadcasted_iota(jnp.int32, (rows, 128), 0)
    rel = lane_k - 64 * (1 - head)
    low = (pos & 255).astype(f32)
    high = (pos - (pos & 255)).astype(f32)
    extra = jnp.where((rel >= 0) & (rel < 3), low, jnp.where((rel >= 3) & (rel < 6), high, 0.0))
    inside = (lane_k // 64) == head
    keys_h = jnp.where(inside, keys.astype(f32), extra).astype(bf16)
    part = jnp.where(rel % 3 == 0, slopes[0], jnp.where(rel % 3 == 1, slopes[1], slopes[2]))
    part = jnp.where((rel >= 0) & (rel < 6), part, 0.0)
    scaled = queries.astype(f32) * 0.125
    queries_h = jnp.where(inside, scaled, part).astype(bf16)
    queries_m = jnp.where(inside, scaled, 0.0).astype(bf16)
    return keys_h, queries_h, queries_m


def score_block(keys_h, queries_h, idx, limit, prefix, slope):
    start = idx * QROWS
    block = queries_h[start : start + QROWS]
    scores = dot_nt(keys_h[:limit], block)
    tail = scores[start:]
    key_pos = start + lax.broadcasted_iota(jnp.int32, tail.shape, 0)
    query_pos = start + lax.broadcasted_iota(jnp.int32, tail.shape, 1)
    ahead = key_pos - query_pos
    tail = tail - (2.0 * slope) * jnp.maximum(ahead, 0).astype(f32)
    tail = jnp.where((ahead <= 0) | (key_pos < prefix), tail, -1e30)
    if start == 0:
        return tail
    return jnp.concatenate([scores[:start], tail], axis=0)


def attend_kernel(tab, prefix, slopes, q_ref, k_ref, v_ref, ctx_ref, ctxt_ref, lse_ref, qs, ks, vs):
    pair = pl.program_id(0)
    length = q_ref.shape[0]
    for blk in range(length // 128):
        where_from = pl.ds(pl.multiple_of(tab[blk], 128), 128)
        rows = slice(blk * 128, blk * 128 + 128)
        qs[rows] = q_ref[where_from, :]
        ks[rows] = k_ref[where_from, :]
        vs[rows] = v_ref[where_from, :]
    values_t = vs[...].astype(f32).T.astype(bf16)
    for head in range(2):
        base = (pair * 2 + head) * 4
        parts = (slopes[base + 1], slopes[base + 2], slopes[base + 3])
        keys_h, queries_h, _ = augmented(head, ks[...], qs[...], parts, 0)
        for idx in range(length // QROWS):
            limit = max((idx + 1) * QROWS, length // 2)
            scores = score_block(keys_h, queries_h, idx, limit, prefix[0], slopes[base])
            top = jnp.max(scores, axis=0, keepdims=True)
            weights = jnp.exp(scores - top)
            total = jnp.sum(weights, axis=0, keepdims=True)
            out = dot_nn(values_t[64 * head : 64 * head + 64, :limit], weights.astype(bf16))
            cols = slice(idx * QROWS, (idx + 1) * QROWS)
            ctxt_ref[64 * head : 64 * head + 64, cols] = out / total
            lse_ref[0, head : head + 1, cols] = top + jnp.log(total)
    ctx = ctxt_ref[...].T.astype(bf16)
    for blk in range(length // 128):
        where_to = pl.ds(pl.multiple_of(tab[blk], 128), 128)
        ctx_ref[where_to, :] = ctx[blk * 128 : blk * 128 + 128]


def attend_back_kernel(
    tab, prefix, slopes, q_ref, k_ref, v_ref, d_ref, ctxt_ref, lse_ref, out_ref, qs, ks, vs, ds, dkv, dqt
):
    pair = pl.program_id(0)
    length = q_ref.shape[0]
    for blk in range(length // 128):
        where_from = pl.ds(pl.multiple_of(tab[blk], 128), 128)
        rows = slice(blk * 128, blk * 128 + 128)
        qs[rows] = q_ref[where_from, :]
        ks[rows] = k_ref[where_from, :]
        vs[rows] = v_ref[where_from, :]
        ds[rows] = d_ref[where_from, :]
    keys_t = ks[...].astype(f32).T.astype(bf16)
    d_ctx = ds[...].astype(f32)
    products = d_ctx.T * ctxt_ref[...]
    inside = lax.broadcasted_iota(jnp.int32, (length, 128), 1) // 64
    dkv[...] = jnp.zeros_like(dkv)
    for head in range(2):
        base = (pair * 2 + head) * 4
        parts = (slopes[base + 1], slopes[base + 2], slopes[base + 3])
        keys_h, queries_h, queries_m = augmented(head, ks[...], qs[...], parts, 0)
        d_head = jnp.where(inside == head, d_ctx, 0.0).astype(bf16)
        delta = jnp.sum(products[64 * head : 64 * head + 64], axis=0, keepdims=True)
        for idx in range(length // QROWS):
            limit = max((idx + 1) * QROWS, length // 2)
            cols = slice(idx * QROWS, (idx + 1) * QROWS)
            scores = score_block(keys_h, queries_h, idx, limit, prefix[0], slopes[base])
            probs = jnp.exp(scores - lse_ref[0, head : head + 1, cols])
            d_probs = dot_nt(vs[:limit], d_head[cols])
            d_scores = (probs * (d_probs - delta[:, cols])).astype(bf16)
            dkv[0, :limit] += dot_nn(d_scores, queries_m[cols])
            dkv[1, :limit] += dot_nn(probs.astype(bf16), d_head[cols])
            dqt[64 * head : 64 * head + 64, cols] = dot_nn(
                keys_t[64 * head : 64 * head + 64, :limit], d_scores
            )
    d_q = (dqt[...].T * 0.125).astype(bf16)
    lanes = [pl.ds(pl.multiple_of(part * 256 + pair * 128, 128), 128) for part in range(3)]
    for blk in range(length // 128):
        where_to = pl.ds(pl.multiple_of(tab[blk], 128), 128)
        rows = slice(blk * 128, blk * 128 + 128)
        out_ref[where_to, lanes[0]] = d_q[rows]
        out_ref[where_to, lanes[1]] = dkv[0, rows].astype(bf16)
        out_ref[where_to, lanes[2]] = dkv[1, rows].astype(bf16)


def smem():
    return pl.BlockSpec(memory_space=pltpu.SMEM)


def column_block(rows, first):
    return pl.BlockSpec((rows, 128), lambda p: (0, first + p))


def attend(tab, prefix, slopes, merged):
    length = merged.shape[0]
    return pl.pallas_call(
        attend_kernel,
        grid=(2,),
        in_specs=[smem(), smem(), smem()] + [column_block(length, 2 * part) for part in range(3)],
        out_specs=[
            column_block(length, 0),
            pl.BlockSpec((128, length), lambda p: (p, 0)),
            pl.BlockSpec((1, 8, length), lambda p: (p, 0, 0)),
        ],
        out_shape=[
            jax.ShapeDtypeStruct((length, 256), bf16),
            jax.ShapeDtypeStruct((256, length), f32),
            jax.ShapeDtypeStruct((2, 8, length), f32),
        ],
        scratch_shapes=[pltpu.VMEM((length, 128), bf16)] * 3,
        cost_estimate=pl.CostEstimate(
            flops=4 * 2 * 2 * 128 * 720896, transcendentals=4 * 720896, bytes_accessed=4 << 20
        ),
        name="attend",
    )(tab, prefix, slopes, merged, merged, merged)


def attend_back(tab, prefix, slopes, merged, d_ctx, ctxt, lse):
    length = merged.shape[0]
    return pl.pallas_call(
        attend_back_kernel,
        grid=(2,),
        in_specs=[smem(), smem(), smem()]
        + [column_block(length, 2 * part) for part in range(3)]
        + [
            column_block(length, 0),
            pl.BlockSpec((128, length), lambda p: (p, 0)),
            pl.BlockSpec((1, 8, length), lambda p: (p, 0, 0)),
        ],
        out_specs=pl.BlockSpec((length, 768), lambda p: (0, 0)),
        out_shape=jax.ShapeDtypeStruct((length, 768), bf16),
        scratch_shapes=[pltpu.VMEM((length, 128), bf16)] * 4
        + [pltpu.VMEM((2, length, 128), f32), pltpu.VMEM((128, length), f32)],
        cost_estimate=pl.CostEstimate(
            flops=4 * 5 * 2 * 128 * 720896, transcendentals=4 * 720896, bytes_accessed=6 << 20
        ),
        name="attend_back",
    )(tab, prefix, slopes, merged, merged, merged, d_ctx, ctxt, lse)


def swap(values, axis):
    return lax.ppermute(values, axis, [(0, 1), (1, 0)])


def place_pairs():
    pairs = []
    for y in range(2):
        for x in range(2):
            for z in range(4):
                for c in range(2):
                    source = ((y * 2 + x) * 4 + z) * 2 + c
                    target = ((y * 2 + (z >> 1)) * 4 + PLACE[2 * x + c]) * 2 + (z & 1)
                    pairs.append((source, target))
    return pairs


def in_order(index, own, other, axis):
    return jnp.where(
        index == 0, jnp.stack([own, other], axis), jnp.stack([other, own], axis)
    )


def gather_group(chunk):
    two = jnp.concatenate([chunk, swap(chunk, "x")], axis=0)
    return jnp.concatenate([two, swap(two, "c")], axis=0)


def scatter_group(left, product):
    half = left.shape[0] // 2
    away = product(left[half:]).astype(bf16)
    came = swap(away, "c")
    kept = product(left[:half]) + came.astype(f32)
    quarter = half // 2
    came_two = swap(kept[quarter:].astype(bf16), "x")
    return kept[:quarter] + came_two.astype(f32)


def gather_blocks(values):
    z_all = lax.all_to_all(
        jnp.broadcast_to(values[None], (4,) + values.shape), "z", 0, 0, tiled=True
    )
    return in_order(lax.axis_index("y"), z_all, swap(z_all, "y"), 0)


def scatter_blocks(values):
    my_y = lax.axis_index("y")
    away = lax.dynamic_index_in_dim(values, 1 - my_y, 0, keepdims=False).astype(bf16)
    kept = lax.dynamic_index_in_dim(values, my_y, 0, keepdims=False)
    half = (kept + swap(away, "y").astype(f32)).astype(bf16)
    return jnp.sum(lax.all_to_all(half, "z", 0, 0, tiled=True).astype(f32), axis=0)


def bring_in(values):
    my_c = lax.axis_index("c")
    kept = lax.dynamic_index_in_dim(values, my_c, 0, keepdims=False)
    away = lax.dynamic_index_in_dim(values, 1 - my_c, 0, keepdims=False)
    both = jnp.concatenate([kept, swap(away, "c")], axis=0)
    return lax.ppermute(both, AXES, place_pairs())


def bring_out(values):
    back = lax.ppermute(values, AXES, [(b, a) for a, b in place_pairs()])
    half = values.shape[0] // 2
    return in_order(lax.axis_index("c"), back[:half], swap(back[half:], "c"), 0)


def small_gather(values):
    z_all = lax.all_to_all(
        jnp.broadcast_to(values[None], (4,) + values.shape), "z", 0, 0, tiled=True
    )
    c_all = in_order(lax.axis_index("c"), z_all, swap(z_all, "c"), 1)
    x_all = in_order(lax.axis_index("x"), c_all, swap(c_all, "x"), 0)
    return in_order(lax.axis_index("y"), x_all, swap(x_all, "y"), 0)


def small_scatter(values):
    for axis, dim in (("c", 3), ("x", 1), ("y", 0)):
        mine = lax.axis_index(axis)
        kept = lax.dynamic_index_in_dim(values, mine, dim, keepdims=False)
        away = lax.dynamic_index_in_dim(values, 1 - mine, dim, keepdims=False)
        values = kept + swap(away, axis)
    return jnp.sum(lax.all_to_all(values, "z", 0, 0, tiled=True), axis=0)


def fast_layer(
    hidden_in,
    out_grad,
    prefix_len,
    alibi_slopes,
    ln1_gain,
    ln1_shift,
    qkv_weight,
    qkv_bias,
    dense_weight,
    dense_bias,
    ln2_gain,
    ln2_shift,
    fc1_weight,
    fc1_bias,
    fc2_weight,
    fc2_bias,
):
    my_x, my_z, my_c = (lax.axis_index(name) for name in ("x", "z", "c"))
    width = hidden_in.shape[2]
    ff_own = fc1_weight.shape[1] // 4

    hidden = bring_in(hidden_in).astype(f32)
    mlp_grad = bring_in(out_grad)

    small = jnp.concatenate(
        [ln1_gain, ln1_shift, dense_bias, ln2_gain, ln2_shift, fc2_bias, qkv_bias, fc1_bias]
    )
    small = lax.reduce_precision(small, 8, 7)
    spare = 512 - small.shape[0]
    small = small_gather(jnp.pad(small, (0, spare)).reshape(4, 128)).reshape(32, 512)
    gain_one, shift_one, dense_vec, gain_two, shift_two, down_vec = (
        small[:, 32 * item : 32 * item + 32].reshape(width) for item in range(6)
    )
    group = 2 * my_c + my_x
    qkv_vec = lax.dynamic_index_in_dim(
        small[:, 192:288].reshape(3, 4, width // 4), group, 1, keepdims=False
    ).reshape(-1)
    up_vec = small[:, 288:416].reshape(2, 2, 4, 2, 128)
    up_vec = lax.dynamic_index_in_dim(up_vec, my_x, 1, keepdims=False)
    up_vec = lax.dynamic_index_in_dim(up_vec, my_c, 2, keepdims=False).reshape(ff_own)

    qkv_cols = qkv_weight.astype(bf16).reshape(32, 3, 2, 2, 256).transpose(3, 2, 0, 1, 4)
    up_cols = fc1_weight.astype(bf16).reshape(32, 2, 2, 4, 2, 128).transpose(2, 4, 0, 1, 3, 5)
    both_cols = jnp.concatenate([qkv_cols.reshape(4, 32, 768), up_cols.reshape(4, 32, ff_own)], axis=2)
    both_cols = lax.all_to_all(both_cols, ("x", "c"), 0, 0, tiled=True)

    def rows_in_order(values):
        cols = values.shape[-1]
        values = values.reshape(2, 4, 2, 64, cols).transpose(0, 2, 1, 3, 4)
        return values.reshape(width, cols)

    qkv_mat = rows_in_order(gather_blocks(both_cols[:, :, :768]))
    dense_all = gather_blocks(dense_weight.astype(bf16))
    dense_kept = lax.dynamic_index_in_dim(dense_all, my_c, 0, keepdims=False)
    dense_away = lax.dynamic_index_in_dim(dense_all, 1 - my_c, 0, keepdims=False)
    dense_mat = in_order(my_c, dense_kept, swap(dense_away, "c"), 1).reshape(256, width)
    up_mat = rows_in_order(gather_blocks(both_cols[:, :, 768:]))
    down_mat = gather_blocks(fc2_weight.astype(bf16)).reshape(ff_own, width)

    from_c = my_z >> 1
    tab = []
    for t in range(4):
        rel = ((t >> 1) ^ my_x) + 2 * ((t & 1) ^ my_c)
        for u in range(2):
            tab.append(rel * 256 + (u ^ from_c) * 128)
    tab = jnp.stack(tab).astype(jnp.int32)
    prefix_all = prefix_all_of(prefix_len)
    prefix = prefix_all.reshape(1)
    slope = lax.dynamic_slice_in_dim(alibi_slopes, 4 * group, 4, 0)
    first = lax.reduce_precision(slope, 8, 7)
    second_part = lax.reduce_precision(slope - first, 8, 7)
    third = lax.reduce_precision(slope - first - second_part, 8, 7)
    slopes = jnp.stack([slope, first, second_part, third], axis=1).reshape(16)

    normed = gather_group(layer_norm(hidden, gain_one, shift_one).astype(bf16))
    merged = (dot_nn(normed, qkv_mat) + qkv_vec).astype(bf16)
    context, context_t, log_total = attend(tab, prefix, slopes, merged)
    second = hidden + scatter_group(context, lambda rows: dot_nn(rows, dense_mat)) + dense_vec
    normed_two = gather_group(layer_norm(second, gain_two, shift_two).astype(bf16))
    pre_act = dot_nn(normed_two, up_mat) + up_vec
    activity = gelu_tanh(pre_act).astype(bf16)
    layer_out = second + scatter_group(activity, lambda rows: dot_nn(rows, down_mat)) + down_vec
    layer_out = bring_out(layer_out.astype(bf16))

    mlp_all = gather_group(mlp_grad)
    out_cot = mlp_grad.astype(f32)
    down_grad = dot_tn(activity, mlp_all)
    down_out = scatter_blocks(down_grad.reshape(2, 4, 128, width))
    ignored, gelu_pull = jax.vjp(gelu_tanh, pre_act)
    pre_grad = gelu_pull(dot_nt(mlp_all, down_mat))[0].astype(bf16)
    up_grad = dot_tn(normed_two, pre_grad)
    ignored, pull_two = jax.vjp(layer_norm, second, gain_two, shift_two)
    norm_grad, gain_two_grad, shift_two_grad = pull_two(
        scatter_group(pre_grad, lambda rows: dot_nt(rows, up_mat))
    )
    second_grad = out_cot + norm_grad
    attn_grad = second_grad.astype(bf16)
    attn_all = gather_group(attn_grad)
    dense_grad = dot_tn(context, attn_all)
    context_grad = dot_nt(attn_all, dense_mat).astype(bf16)
    merged_grad = attend_back(tab, prefix, slopes, merged, context_grad, context_t, log_total)
    qkv_grad = dot_tn(normed, merged_grad)
    ignored, pull_one = jax.vjp(layer_norm, hidden, gain_one, shift_one)
    first_grad, gain_one_grad, shift_one_grad = pull_one(
        scatter_group(merged_grad, lambda rows: dot_nt(rows, qkv_mat))
    )
    input_grad = bring_out((second_grad + first_grad).astype(bf16))

    def rows_of_owner(values):
        cols = values.shape[-1]
        return values.reshape(2, 2, 4, 64, cols).transpose(0, 2, 1, 3, 4).reshape(2, 4, 4, 32, cols)

    up_rows = scatter_blocks(rows_of_owner(up_grad)).astype(bf16)
    qkv_rows = scatter_blocks(rows_of_owner(qkv_grad)).astype(bf16)
    both_rows = jnp.concatenate([qkv_rows, up_rows], axis=2)
    both_rows = lax.all_to_all(both_rows, ("x", "c"), 0, 0, tiled=True).astype(f32)
    qkv_out = both_rows[:, :, :768].reshape(2, 2, 32, 3, 256).transpose(2, 3, 1, 0, 4)
    up_out = both_rows[:, :, 768:].reshape(2, 2, 32, 2, 4, 128).transpose(2, 3, 0, 4, 1, 5)

    dense_rows = dense_grad.reshape(4, 2, 32, width)
    dense_mine = lax.dynamic_index_in_dim(dense_rows, my_c, 1, keepdims=False)
    dense_away = lax.dynamic_index_in_dim(dense_rows, 1 - my_c, 1, keepdims=False)
    dense_came = swap(dense_away.astype(bf16), "c").astype(f32)
    dense_out = scatter_blocks(in_order(my_c, dense_mine, dense_came, 0))

    qkv_vec_grad = jnp.zeros((3, 4, width // 4), f32)
    qkv_vec_grad = lax.dynamic_update_slice(
        qkv_vec_grad, column_sum(merged_grad).reshape(3, 1, width // 4), (0, group, 0)
    )
    up_vec_grad = jnp.zeros((2, 2, 4, 2, 128), f32)
    up_vec_grad = lax.dynamic_update_slice(
        up_vec_grad, column_sum(pre_grad).reshape(2, 1, 4, 1, 128), (0, my_x, 0, my_c, 0)
    )
    vectors = [
        gain_one_grad,
        shift_one_grad,
        column_sum(attn_grad),
        gain_two_grad,
        shift_two_grad,
        column_sum(mlp_grad),
        qkv_vec_grad,
        up_vec_grad,
    ]
    small_grads = jnp.concatenate(
        [item.reshape(32, -1) for item in vectors] + [jnp.zeros((32, spare), f32)], axis=1
    )
    small_out = small_scatter(small_grads.reshape(2, 2, 4, 2, 4, 128)).reshape(512)
    own = [small_out[32 * item : 32 * item + 32] for item in range(6)]
    return (
        layer_out,
        input_grad,
        own[0],
        own[1],
        qkv_out.reshape(32, 3 * width),
        small_out[192:288],
        dense_out,
        own[2],
        own[3],
        own[4],
        up_out.reshape(32, 4 * ff_own),
        small_out[288:416],
        down_out,
        own[5],
    )


def prefix_all_of(prefix_len):
    my_c = lax.axis_index("c")
    return lax.ppermute(
        lax.dynamic_index_in_dim(prefix_len, my_c, 0).astype(f32), AXES, place_pairs()
    ).astype(jnp.int32)


def fast(mesh):
    split = Mesh(mesh.devices.reshape(2, 2, 4, 2), AXES)
    tokens = P(("y", "x"), ("z", "c"), None)
    matrix, vector = P(AXES, None), P(AXES)
    weights = (vector, vector, matrix, vector, matrix, vector, vector, vector, matrix, vector, matrix, vector)
    return jax.shard_map(
        fast_layer,
        mesh=split,
        in_specs=(tokens, tokens, P(("y", "x")), P()) + weights,
        out_specs=(tokens, tokens) + weights,
        check_vma=False,
    )


def solution(mesh):
    if tuple(mesh.shape[name] for name in ("dp", "seq")) == (4, 8):
        return fast(mesh)
    return general(mesh)
```
